1024 devices in a mesh: shell: 8 (over x, core), tile: 128 (over z, y).
Axes of the slice: x: 4, y: 4, z: 32, core: 2. Of those that a mesh axis runs over, the one named last changes fastest.
Arguments:
- residual: bfloat16 [32, 2097152], P('shell', 'tile'), may hold values from -6 to 6
- tile_ray: int32 [16384], P('tile'), may hold values from 0 to 127, as said below
- filter_rows: bfloat16 [128, 128], replicated, may hold values from -0.5 to 0.5
- filter_cols: bfloat16 [128, 128], replicated, may hold values from -0.5 to 0.5
- band_lo: int32 [32], replicated, may hold values from 0 to 16
- shell_weight: float32 [32], replicated, may hold values from 0.3 to 3
Outputs:
- shell_grad: bfloat16 [32, 2097152], P('shell', 'tile')
The draws below stay inside these ranges and needn't reach their ends.
Inputs may be any that keep to these rules, and one draw needn't show every extreme that they name: `tile_ray`: for each tile t, entries t * 128 to (t + 1) * 128 - 1 are a permutation of 0 to 127.
All inputs are finite; a program needn't handle non-finite values.
Results may differ from the reference program's by a relative error of at most 0.006.
Values may be sent and summed in bfloat16 or wider, within the bound.
No kernel may reach another device: no remote copies, remote signals or barrier semaphores. Data moves between devices by JAX's collectives and lax.ppermute only.
A program may use at most 32 MiB of HBM per device.

```python
import math
import jax
import jax.numpy as jnp
from jax import lax

TILE_SIDE = 128
RAY_DEV = 16384
SHELLS = 32
BAND = 16
RAYS = 2097152
N_TILE = 128


def draw_tile_ray(key, part):
    keys = jax.random.split(jax.random.fold_in(key, 11), N_TILE)
    orders = jax.vmap(lambda single: jax.random.permutation(single, TILE_SIDE))(keys)
    return orders.reshape(-1).astype(jnp.int32)


def place_ends(result, own_key, low, largest):
    extent = result.shape
    spot = [jax.random.randint(jax.random.fold_in(own_key, axis), (), 0, extent[axis]) for axis in range(len(extent))]
    result = result.at[tuple(spot)].set(low)
    longest = extent.index(max(extent))
    spot[longest] = (spot[longest] + 1) % extent[longest]
    return result.at[tuple(spot)].set(largest)


def steps_of(stream_key, dims, cuts, smallest, top_value):
    gain = 1.0
    for dim, blocks in cuts:
        steps = jax.random.uniform(jax.random.fold_in(jax.random.fold_in(stream_key, 6), dim), (blocks,), jnp.float32, smallest / len(cuts), top_value / len(cuts))
        gain = gain * jnp.repeat(jnp.exp(steps), dims[dim] // blocks).reshape((-1,) + (1,) * (len(dims) - 1 - dim))
    return gain


def gaussian(stream_key, extent, deviation, limit, shards=(), held_as=jnp.bfloat16):
    values = deviation * jax.random.normal(stream_key, extent, jnp.float32)
    if shards:
        values = values * steps_of(stream_key, extent, shards, -0.22, 0.18)
    return jnp.clip(values, -limit, limit).astype(held_as)


def setup_inputs(seed: int = 0) -> dict:
    streams_of = jax.random.split(jax.random.key(seed), 7)
    return {
        "residual": gaussian(streams_of[0], (SHELLS, RAYS), 1.0, 6.0, ((0, 8), (1, 128))),
        "tile_ray": draw_tile_ray(jax.random.fold_in(streams_of[6], 71), 0),
        "filter_rows": gaussian(streams_of[2], (TILE_SIDE, TILE_SIDE), TILE_SIDE ** -0.5, 0.5),
        "filter_cols": gaussian(streams_of[3], (TILE_SIDE, TILE_SIDE), TILE_SIDE ** -0.5, 0.5),
        "band_lo": place_ends(jax.random.randint(streams_of[4], (SHELLS,), 0, SHELLS - BAND + 1), jax.random.fold_in(streams_of[4], 1), 0, SHELLS - BAND).astype(jnp.int32),
        "shell_weight": jnp.clip(jnp.exp(jax.random.uniform(streams_of[5], (SHELLS,), jnp.float32, math.log(0.3), math.log(3.0))), 0.3, 3.0),
    }


def kernel_table(band_lo, shell_weight):
    count = shell_weight.shape[0]
    band = count // 2
    index = jnp.arange(count)
    chi_shell = (index.astype(jnp.float32) + 0.5) / count
    chi_source = (band_lo.astype(jnp.float32) + band) / count
    inside = (index[None, :] >= band_lo[:, None]) & (index[None, :] < band_lo[:, None] + band)
    values = 8.0 * shell_weight[None, :] * chi_shell[None, :] * (chi_source[:, None] - chi_shell[None, :]) / chi_source[:, None]
    return jnp.where(inside, values, jnp.zeros_like(values)).astype(jnp.bfloat16)


def reference(residual, tile_ray, filter_rows, filter_cols, band_lo, shell_weight):
    planes = residual.shape[0]
    ntile = N_TILE
    run = RAY_DEV // ntile
    side = filter_rows.shape[0]
    received = residual.reshape(planes, ntile, ntile, run).transpose(0, 2, 1, 3).reshape(planes, ntile, side, side)
    order = jnp.broadcast_to(tile_ray.reshape(1, ntile, side, 1), received.shape)
    pixels = jnp.take_along_axis(received, order, axis=2)
    image = pixels.astype(jnp.float32)
    half = jnp.einsum("stik,kb->stib", image, filter_cols.astype(jnp.float32), precision=lax.Precision.HIGHEST)
    whole = jnp.einsum("ia,stib->stab", filter_rows.astype(jnp.float32), half, precision=lax.Precision.HIGHEST)
    smoothed = whole.astype(jnp.bfloat16).reshape(planes, ntile * RAY_DEV)
    kernel = kernel_table(band_lo, shell_weight)
    return jnp.dot(kernel.T, smoothed, preferred_element_type=jnp.float32).astype(jnp.bfloat16)
```

```python
import jax
import jax.numpy as jnp
from jax import lax
from jax.experimental import pallas as pl
from jax.experimental.pallas import tpu as pltpu
from jax.sharding import PartitionSpec as P

VMEM = pl.BlockSpec(memory_space=pltpu.VMEM)
TRIM = pltpu.CompilerParams(vmem_limit_bytes=16 * 2**20)
ROW_BY_ROW = (((1,), (1,)), ((), ()))


def iota(shape, axis):
    return lax.broadcasted_iota(jnp.int32, shape, axis)


def tables_kernel(groups, band_ref, weight_ref, ray_ref, rows_ref, mix_ref, smooth_ref):
    count = band_ref.shape[1]
    per = count // groups
    band = count // 2
    size = mix_ref.shape[0]
    run = size // groups
    shell = iota((count, count), 0)
    plane = iota((count, count), 1)
    low = jnp.broadcast_to(band_ref[...], (count, count))
    lanes = jnp.broadcast_to(weight_ref[...], (count, count))
    weight = jnp.sum(jnp.where(shell == plane, lanes, 0.0), axis=1, keepdims=True)
    chi_shell = (shell.astype(jnp.float32) + 0.5) / count
    chi_source = (low.astype(jnp.float32) + band) / count
    values = 8.0 * weight * chi_shell * (chi_source - chi_shell) / chi_source
    inside = (shell >= low) & (shell < low + band)
    table = jnp.where(inside, values, 0.0).astype(jnp.bfloat16)
    spot = iota((size, count), 0)
    pick = (iota((size, count), 1) == spot // run * per + spot % per).astype(jnp.bfloat16)
    by_shell = jnp.dot(pick, table, preferred_element_type=jnp.float32).astype(jnp.bfloat16)
    full = lax.dot_general(by_shell, pick, ROW_BY_ROW, preferred_element_type=jnp.float32)
    here, there = iota((size, size), 0), iota((size, size), 1)
    mix_ref[...] = jnp.where(here % run // per == there % run // per, full, 0.0).astype(jnp.bfloat16)

    side = rows_ref.shape[0]
    each = smooth_ref.shape[0] // side
    wide = iota((side * each, side), 0) // each
    pixel = (iota((side * each, side), 1) == wide).astype(jnp.bfloat16)
    spread = lax.dot_general(pixel, rows_ref[...], ROW_BY_ROW, preferred_element_type=jnp.float32).astype(jnp.bfloat16)
    source = (ray_ref[...] == wide).astype(jnp.bfloat16)
    product = lax.dot_general(spread, source, ROW_BY_ROW, preferred_element_type=jnp.float32)
    smooth_ref[...] = jnp.where(here % each == there % each, product, 0.0).astype(jnp.bfloat16)


def mix_kernel(mix_ref, planes_ref, out_ref):
    out_ref[...] = jnp.dot(mix_ref[...], planes_ref[...], preferred_element_type=jnp.float32).astype(jnp.bfloat16)


def smooth_kernel(smooth_ref, cols_ref, pixels_ref, out_ref):
    half = jnp.dot(pixels_ref[...], cols_ref[...], preferred_element_type=jnp.float32)
    upper = half.astype(jnp.bfloat16)
    lower = (half - upper.astype(jnp.float32)).astype(jnp.bfloat16)
    whole = jnp.dot(smooth_ref[...], upper, preferred_element_type=jnp.float32)
    whole += jnp.dot(smooth_ref[...], lower, preferred_element_type=jnp.float32)
    out_ref[...] = whole.astype(jnp.bfloat16)


def shards(residual, tile_ray, filter_rows, filter_cols, band_lo, shell_weight):
    planes, rays = residual.shape
    groups = lax.axis_size("shell")
    ntile = lax.axis_size("tile")
    run = rays // ntile
    lines = planes * ntile
    square = jax.ShapeDtypeStruct((lines, lines), jnp.bfloat16)
    slab = jax.ShapeDtypeStruct((lines, run), jnp.bfloat16)

    mix, smooth = pl.pallas_call(
        lambda *refs: tables_kernel(groups, *refs), out_shape=(square, square), in_specs=[VMEM] * 4, out_specs=(VMEM, VMEM), compiler_params=TRIM, name="tables"
    )(band_lo.reshape(1, -1), shell_weight.reshape(1, -1), tile_ray.reshape(1, -1), filter_rows)

    by_tile = residual.reshape(planes, groups, ntile // groups, run)
    spread = lax.all_to_all(by_tile, "shell", 1, 1, tiled=True).transpose(1, 2, 0, 3).reshape(lines, run)
    mixed = pl.pallas_call(mix_kernel, out_shape=slab, in_specs=[VMEM] * 2, out_specs=VMEM, compiler_params=TRIM, name="mix")(mix, spread)
    own = lax.all_to_all(mixed.reshape(groups, lines // groups, run), "shell", 0, 0, tiled=True)
    pixels = lax.all_to_all(own.reshape(ntile, planes, run), "tile", 0, 0, tiled=True)
    whole = pl.pallas_call(smooth_kernel, out_shape=slab, in_specs=[VMEM] * 3, out_specs=VMEM, compiler_params=TRIM, name="smooth")(smooth, filter_cols, pixels.reshape(lines, run))
    return whole.reshape(ntile, planes, run).transpose(1, 0, 2).reshape(planes, rays)


def solution(mesh):
    in_specs = (P("shell", "tile"), P("tile"), P(), P(), P(), P())
    out_specs = P("shell", "tile")
    return jax.shard_map(shards, mesh=mesh, in_specs=in_specs, out_specs=out_specs, check_vma=False)
```

```python
import jax
import jax.numpy as jnp
from jax import lax
from jax.experimental import pallas as pl
from jax.experimental.pallas import tpu as pltpu
from jax.sharding import PartitionSpec as P

VMEM = pl.BlockSpec(memory_space=pltpu.VMEM)
TRIM = pltpu.CompilerParams(vmem_limit_bytes=16 * 2**20)
ROW_BY_ROW = (((1,), (1,)), ((), ()))


def iota(shape, axis):
    return lax.broadcasted_iota(jnp.int32, shape, axis)


def tables_kernel(groups, ys, band_ref, weight_ref, ray_ref, rows_ref, mix_ref, smooth_ref):
    count = band_ref.shape[1]
    per = count // groups
    band = count // 2
    size = mix_ref.shape[0]
    run = size // groups
    shell = iota((count, count), 0)
    plane = iota((count, count), 1)
    low = jnp.broadcast_to(band_ref[...], (count, count))
    lanes = jnp.broadcast_to(weight_ref[...], (count, count))
    weight = jnp.sum(jnp.where(shell == plane, lanes, 0.0), axis=1, keepdims=True)
    chi_shell = (shell.astype(jnp.float32) + 0.5) / count
    chi_source = (low.astype(jnp.float32) + band) / count
    values = 8.0 * weight * chi_shell * (chi_source - chi_shell) / chi_source
    inside = (shell >= low) & (shell < low + band)
    table = jnp.where(inside, values, 0.0).astype(jnp.bfloat16)
    spot, which = iota((size, count), 0), iota((size, count), 1)
    part = run // ys
    pick_out = (which == spot // part % groups * per + spot % per).astype(jnp.bfloat16)
    pick_in = (which == spot // run * per + spot % per).astype(jnp.bfloat16)
    by_shell = jnp.dot(pick_out, table, preferred_element_type=jnp.float32).astype(jnp.bfloat16)
    full = lax.dot_general(by_shell, pick_in, ROW_BY_ROW, preferred_element_type=jnp.float32)
    here, there = iota((size, size), 0), iota((size, size), 1)
    tile_out = here % part // per * ys + here // (part * groups)
    mix_ref[...] = jnp.where(tile_out == there % run // per, full, 0.0).astype(jnp.bfloat16)

    side = rows_ref.shape[0]
    each = smooth_ref.shape[0] // side
    wide = iota((side * each, side), 0) // each
    pixel = (iota((side * each, side), 1) == wide).astype(jnp.bfloat16)
    spread = lax.dot_general(pixel, rows_ref[...], ROW_BY_ROW, preferred_element_type=jnp.float32).astype(jnp.bfloat16)
    source = (ray_ref[...] == wide).astype(jnp.bfloat16)
    product = lax.dot_general(spread, source, ROW_BY_ROW, preferred_element_type=jnp.float32)
    smooth_ref[...] = jnp.where(here % each == there % each, product, 0.0).astype(jnp.bfloat16)


def mix_kernel(mix_ref, planes_ref, out_ref):
    out_ref[...] = jnp.dot(mix_ref[...], planes_ref[...], preferred_element_type=jnp.float32).astype(jnp.bfloat16)


def smooth_kernel(smooth_ref, cols_ref, pixels_ref, out_ref):
    half = jnp.dot(pixels_ref[...], cols_ref[...], preferred_element_type=jnp.float32)
    upper = half.astype(jnp.bfloat16)
    lower = (half - upper.astype(jnp.float32)).astype(jnp.bfloat16)
    whole = jnp.dot(smooth_ref[...], upper, preferred_element_type=jnp.float32)
    whole += jnp.dot(smooth_ref[...], lower, preferred_element_type=jnp.float32)
    out_ref[...] = whole.astype(jnp.bfloat16)


def shards(residual, tile_ray, filter_rows, filter_cols, band_lo, shell_weight):
    planes, rays = residual.shape
    groups = lax.axis_size("shell")
    zs, ys = lax.axis_size("z"), lax.axis_size("y")
    ntile = zs * ys
    run = rays // ntile
    lines = planes * ntile
    square = jax.ShapeDtypeStruct((lines, lines), jnp.bfloat16)
    slab = jax.ShapeDtypeStruct((lines, run), jnp.bfloat16)

    mix, smooth = pl.pallas_call(
        lambda *refs: tables_kernel(groups, ys, *refs), out_shape=(square, square), in_specs=[VMEM] * 4, out_specs=(VMEM, VMEM), compiler_params=TRIM, name="tables"
    )(band_lo.reshape(1, -1), shell_weight.reshape(1, -1), tile_ray.reshape(1, -1), filter_rows)

    by_tile = residual.reshape(planes, groups, ntile // groups, run)
    spread = lax.all_to_all(by_tile, "shell", 1, 1, tiled=True).transpose(1, 2, 0, 3).reshape(lines, run)
    mixed = pl.pallas_call(mix_kernel, out_shape=slab, in_specs=[VMEM] * 2, out_specs=VMEM, compiler_params=TRIM, name="mix")(mix, spread)
    own = lax.all_to_all(mixed.reshape(ys * groups, -1, run), ("y", "shell"), 0, 0, tiled=True)
    pixels = lax.all_to_all(own.reshape(ys, zs, planes, run), "z", 1, 1, tiled=True).transpose(1, 0, 2, 3)
    whole = pl.pallas_call(smooth_kernel, out_shape=slab, in_specs=[VMEM] * 3, out_specs=VMEM, compiler_params=TRIM, name="smooth")(smooth, filter_cols, pixels.reshape(lines, run))
    return whole.reshape(ntile, planes, run).transpose(1, 0, 2).reshape(planes, rays)


def solution(mesh):
    mesh = jax.sharding.Mesh(mesh.devices.reshape(8, 32, 4), ("shell", "z", "y"))
    in_specs = (P("shell", ("z", "y")), P(("z", "y")), P(), P(), P(), P())
    out_specs = P("shell", ("z", "y"))
    return jax.shard_map(shards, mesh=mesh, in_specs=in_specs, out_specs=out_specs, check_vma=False)
```

```python
import jax
import jax.numpy as jnp
from jax import lax
from jax.experimental import pallas as pl
from jax.experimental.pallas import tpu as pltpu
from jax.sharding import Mesh, PartitionSpec as P

VMEM = pl.BlockSpec(memory_space=pltpu.VMEM)
TRIM = pltpu.CompilerParams(vmem_limit_bytes=16 * 2**20)
ROW_BY_ROW = (((1,), (1,)), ((), ()))
BF16 = jnp.bfloat16
F32 = jnp.float32

X, CORE, Z, Y = 4, 2, 32, 4
SHELL = X * CORE
SIDE = 128
PER = 4
PART = SIDE // X
ZR = Z // X
LINES = PER * Z * Y


def iota(shape, axis):
    return lax.broadcasted_iota(jnp.int32, shape, axis)


def one_hot(match):
    return match.astype(BF16)


def dot(a, b):
    return jnp.dot(a, b, preferred_element_type=F32)


def tables_kernel(band_ref, weight_ref, ray_ref, rows_ref, cols_ref, mix_ref, smooth_ref, wide_ref):
    count = SHELL * PER
    band = count // 2
    core = lax.axis_index("core")
    shell, plane = iota((count, count), 0), iota((count, count), 1)
    low = jnp.broadcast_to(band_ref[...], (count, count))
    lanes = jnp.broadcast_to(weight_ref[...], (count, count))
    weight = jnp.sum(jnp.where(shell == plane, lanes, 0.0), axis=1, keepdims=True)
    chi_shell = (shell.astype(F32) + 0.5) / count
    chi_source = (low.astype(F32) + band) / count
    values = 8.0 * weight * chi_shell * (chi_source - chi_shell) / chi_source
    inside = (shell >= low) & (shell < low + band)
    table = jnp.where(inside, values, 0.0).astype(BF16)

    spot, which = iota((LINES, count), 0), iota((LINES, count), 1)
    pick_out = one_hot(which == (spot // SIDE * CORE + core) * PER + spot % PER)
    spot, which = iota((CORE * LINES, count), 0), iota((CORE * LINES, count), 1)
    pick_in = one_hot(which == spot // SIDE * PER + spot % PER)
    full = lax.dot_general(dot(pick_out, table).astype(BF16), pick_in, ROW_BY_ROW, preferred_element_type=F32)
    here, there = iota((LINES, CORE * LINES), 0), iota((LINES, CORE * LINES), 1)
    mix_ref[...] = jnp.where(here % SIDE // PER == there % SIDE // PER, full, 0.0).astype(BF16)

    line, lane = iota((LINES, SIDE), 0), iota((LINES, SIDE), 1)
    spread = lax.dot_general(one_hot(lane == line // PER), rows_ref[...], ROW_BY_ROW, preferred_element_type=F32).astype(BF16)
    source = one_hot(ray_ref[...] == line % SIDE // PER * Y + line // SIDE)
    product = lax.dot_general(spread, source, ROW_BY_ROW, preferred_element_type=F32)
    here, there = iota((LINES, LINES), 0), iota((LINES, LINES), 1)
    smooth_ref[...] = jnp.where(here % PER == there % PER, product, 0.0).astype(BF16)

    cols = dot(one_hot(lane == line // SIDE * PART + line % PART), cols_ref[...])
    for y in range(Y):
        wide_ref[:, y * SIDE : (y + 1) * SIDE] = jnp.where(line % SIDE // PART == y, cols, 0.0).astype(BF16)


def swap(slabs):
    return [jnp.concatenate([s[:, k * PART : (k + 1) * PART] for s in slabs], axis=1) for k in range(X)]


def send_kernel(rays_ref, out_ref):
    rays = rays_ref[...]
    wide = jnp.concatenate([rays[k * SIDE : (k + 1) * SIDE] for k in range(X)], axis=1)
    to, at = iota((SIDE, SIDE), 0), iota((SIDE, SIDE), 1)
    run = ZR * PER
    order = one_hot(at == to % run // PER * (Y * PER) + to // run * PER + to % PER)
    turned = dot(order, wide)
    for x, slab in enumerate(swap([turned[:, k * SIDE : (k + 1) * SIDE] for k in range(X)])):
        slab = slab.astype(BF16)
        for core in range(CORE):
            at_row = (x * CORE + core) * SIDE
            out_ref[at_row : at_row + SIDE] = slab


def mix_kernel(mix_ref, planes_ref, out_ref):
    mixed = dot(mix_ref[...], planes_ref[...])
    run = ZR * PER
    for x in range(X):
        rows = [mixed[x * SIDE + y * run : x * SIDE + (y + 1) * run] for y in range(Y)]
        for k, slab in enumerate(swap(rows)):
            at_row = x * SIDE + k * run
            out_ref[at_row : at_row + run] = slab.astype(BF16)


def smooth_kernel(smooth_ref, wide_ref, pixels_ref, out_ref):
    pixels = pixels_ref[...]
    flat = jnp.concatenate([pixels[x * SIDE : (x + 1) * SIDE] for x in range(X)], axis=1)
    half = dot(flat, wide_ref[...])
    half = jnp.concatenate([half[:, y * SIDE : (y + 1) * SIDE] for y in range(Y)], axis=0)
    upper = half.astype(BF16)
    lower = (half - upper.astype(F32)).astype(BF16)
    out_ref[...] = (dot(smooth_ref[...], upper) + dot(smooth_ref[...], lower)).astype(BF16)


def call(kernel, name, shapes, *args):
    outs = [jax.ShapeDtypeStruct(shape, BF16) for shape in shapes]
    specs = {"in_specs": [VMEM] * len(args), "out_specs": [VMEM] * len(shapes)}
    return pl.pallas_call(kernel, out_shape=outs, compiler_params=TRIM, name=name, **specs)(*args)


def shards(residual, tile_ray, filter_rows, filter_cols, band_lo, shell_weight):
    tiles = Z * Y
    mix, smooth, wide = call(
        tables_kernel, "tables", [(LINES, CORE * LINES), (LINES, LINES), (LINES, LINES)],
        band_lo.reshape(1, -1), shell_weight.reshape(1, -1), tile_ray.reshape(1, -1), filter_rows, filter_cols,
    )
    rays = residual.reshape(PER, tiles, SIDE).transpose(1, 0, 2).reshape(LINES, SIDE)
    (send,) = call(send_kernel, "send", [(CORE * LINES, SIDE)], rays)
    peers = SHELL * Y
    planes = lax.all_to_all(send.reshape(peers, -1, SIDE), ("x", "core", "y"), 0, 0, tiled=True)
    (mixed,) = call(mix_kernel, "mix", [(LINES, SIDE)], mix, planes.reshape(CORE * LINES, SIDE))
    pixels = lax.all_to_all(mixed.reshape(X * Z, PER, SIDE), ("x", "z"), 0, 0, tiled=True)
    (whole,) = call(smooth_kernel, "smooth", [(LINES, SIDE)], smooth, wide, pixels.reshape(LINES, SIDE))
    return whole.reshape(tiles, PER, SIDE).transpose(1, 0, 2).reshape(PER, tiles * SIDE)


def solution(mesh):
    mesh = Mesh(mesh.devices.reshape(X, CORE, Z, Y), ("x", "core", "z", "y"))
    slab = P(("x", "core"), ("z", "y"))
    in_specs = (slab, P(("z", "y")), P(), P(), P(), P())
    return jax.shard_map(shards, mesh=mesh, in_specs=in_specs, out_specs=slab, check_vma=False)
```

```python
import jax
import jax.numpy as jnp
from jax import lax
from jax.experimental import pallas as pl
from jax.experimental.pallas import tpu as pltpu
from jax.sharding import Mesh, PartitionSpec as P

VMEM = pl.BlockSpec(memory_space=pltpu.VMEM)
TRIM = pltpu.CompilerParams(vmem_limit_bytes=16 * 2**20)
ROW_BY_ROW = (((1,), (1,)), ((), ()))
BF16 = jnp.bfloat16
F32 = jnp.float32

X, CORE, Z, Y = 4, 2, 32, 4
SHELL = X * CORE
SIDE = 128
PER = 4
PART = SIDE // X
ZR = Z // X
LINES = PER * Z * Y
FIRST = 17


def iota(shape, axis):
    return lax.broadcasted_iota(jnp.int32, shape, axis)


def one_hot(match):
    return match.astype(BF16)


def dot(a, b):
    return jnp.dot(a, b, preferred_element_type=F32)


def tables_kernel(band_ref, weight_ref, ray_ref, rows_ref, cols_ref, mix_ref, smooth_ref, wide_ref):
    count = SHELL * PER
    band = count // 2
    core = lax.axis_index("core")
    shell, plane = iota((count, count), 0), iota((count, count), 1)
    low = jnp.broadcast_to(band_ref[...], (count, count))
    lanes = jnp.broadcast_to(weight_ref[...], (count, count))
    weight = jnp.sum(jnp.where(shell == plane, lanes, 0.0), axis=1, keepdims=True)
    chi_shell = (shell.astype(F32) + 0.5) / count
    chi_source = (low.astype(F32) + band) / count
    values = 8.0 * weight * chi_shell * (chi_source - chi_shell) / chi_source
    inside = (shell >= low) & (shell < low + band)
    table = jnp.where(inside, values, 0.0).astype(BF16)

    spot, which = iota((LINES, count), 0), iota((LINES, count), 1)
    pick_out = one_hot(which == (spot // SIDE * CORE + core) * PER + spot % PER)
    spot, which = iota((CORE * LINES, count), 0), iota((CORE * LINES, count), 1)
    pick_in = one_hot(which == spot // SIDE * PER + spot % PER)
    full = lax.dot_general(dot(pick_out, table).astype(BF16), pick_in, ROW_BY_ROW, preferred_element_type=F32)
    here, there = iota((LINES, CORE * LINES), 0), iota((LINES, CORE * LINES), 1)
    mix_ref[...] = jnp.where(here % SIDE // PER == there % SIDE // PER, full, 0.0).astype(BF16)

    line, lane = iota((LINES, SIDE), 0), iota((LINES, SIDE), 1)
    spread = lax.dot_general(one_hot(lane == line // PER), rows_ref[...], ROW_BY_ROW, preferred_element_type=F32).astype(BF16)
    source = one_hot(ray_ref[...] == (line % SIDE // PER + FIRST) % Z * Y + line // SIDE)
    product = lax.dot_general(spread, source, ROW_BY_ROW, preferred_element_type=F32)
    here, there = iota((LINES, LINES), 0), iota((LINES, LINES), 1)
    smooth_ref[...] = jnp.where(here % PER == there % PER, product, 0.0).astype(BF16)

    cols = dot(one_hot(lane == line // SIDE * PART + line % PART), cols_ref[...])
    for y in range(Y):
        wide_ref[:, y * SIDE : (y + 1) * SIDE] = jnp.where(line % SIDE // PART == y, cols, 0.0).astype(BF16)


def swap(slabs):
    return [jnp.concatenate([s[:, k * PART : (k + 1) * PART] for s in slabs], axis=1) for k in range(X)]


def send_kernel(rays_ref, out_ref):
    cut = FIRST * Y * PER
    rays = jnp.concatenate([rays_ref[cut:], rays_ref[:cut]], axis=0)
    wide = jnp.concatenate([rays[k * SIDE : (k + 1) * SIDE] for k in range(X)], axis=1)
    to, at = iota((SIDE, SIDE), 0), iota((SIDE, SIDE), 1)
    run = ZR * PER
    order = one_hot(at == to % run // PER * (Y * PER) + to // run * PER + to % PER)
    turned = dot(order, wide)
    for x, slab in enumerate(swap([turned[:, k * SIDE : (k + 1) * SIDE] for k in range(X)])):
        slab = slab.astype(BF16)
        for core in range(CORE):
            at_row = (x * CORE + core) * SIDE
            out_ref[at_row : at_row + SIDE] = slab


def mix_kernel(mix_ref, planes_ref, out_ref):
    mixed = dot(mix_ref[...], planes_ref[...])
    run = ZR * PER
    for x in range(X):
        rows = [mixed[x * SIDE + y * run : x * SIDE + (y + 1) * run] for y in range(Y)]
        for k, slab in enumerate(swap(rows)):
            at_row = x * SIDE + k * run
            out_ref[at_row : at_row + run] = slab.astype(BF16)


def smooth_kernel(smooth_ref, wide_ref, pixels_ref, out_ref):
    pixels = pixels_ref[...]
    flat = jnp.concatenate([pixels[x * SIDE : (x + 1) * SIDE] for x in range(X)], axis=1)
    half = dot(flat, wide_ref[...])
    half = jnp.concatenate([half[:, y * SIDE : (y + 1) * SIDE] for y in range(Y)], axis=0)
    upper = half.astype(BF16)
    lower = (half - upper.astype(F32)).astype(BF16)
    out_ref[...] = (dot(smooth_ref[...], upper) + dot(smooth_ref[...], lower)).astype(BF16)


def call(kernel, name, shapes, *args):
    outs = [jax.ShapeDtypeStruct(shape, BF16) for shape in shapes]
    specs = {"in_specs": [VMEM] * len(args), "out_specs": [VMEM] * len(shapes)}
    return pl.pallas_call(kernel, out_shape=outs, compiler_params=TRIM, name=name, **specs)(*args)


def shards(residual, tile_ray, filter_rows, filter_cols, band_lo, shell_weight):
    tiles = Z * Y
    mix, smooth, wide = call(
        tables_kernel, "tables", [(LINES, CORE * LINES), (LINES, LINES), (LINES, LINES)],
        band_lo.reshape(1, -1), shell_weight.reshape(1, -1), tile_ray.reshape(1, -1), filter_rows, filter_cols,
    )
    rays = residual.reshape(PER, tiles, SIDE).transpose(1, 0, 2).reshape(LINES, SIDE)
    (send,) = call(send_kernel, "send", [(CORE * LINES, SIDE)], rays)
    peers = SHELL * Y
    planes = lax.all_to_all(send.reshape(peers, -1, SIDE), ("x", "core", "y"), 0, 0, tiled=True)
    (mixed,) = call(mix_kernel, "mix", [(LINES, SIDE)], mix, planes.reshape(CORE * LINES, SIDE))
    members = [[x * Z + (FIRST + z) % Z for x in range(X) for z in range(Z)]]
    pixels = lax.all_to_all(
        mixed.reshape(X * Z, PER, SIDE), ("x", "z"), 0, 0, axis_index_groups=members, tiled=True
    )
    (whole,) = call(smooth_kernel, "smooth", [(LINES, SIDE)], smooth, wide, pixels.reshape(LINES, SIDE))
    return whole.reshape(tiles, PER, SIDE).transpose(1, 0, 2).reshape(PER, tiles * SIDE)


def solution(mesh):
    mesh = Mesh(mesh.devices.reshape(X, CORE, Z, Y), ("x", "core", "z", "y"))
    slab = P(("x", "core"), ("z", "y"))
    in_specs = (slab, P(("z", "y")), P(), P(), P(), P())
    return jax.shard_map(shards, mesh=mesh, in_specs=in_specs, out_specs=slab, check_vma=False)
```

```python
import jax
import jax.numpy as jnp
from jax import lax
from jax.experimental import pallas as pl
from jax.experimental.pallas import tpu as pltpu
from jax.sharding import Mesh, PartitionSpec as P

VMEM = pl.BlockSpec(memory_space=pltpu.VMEM)
HBM = pl.BlockSpec(memory_space=pltpu.HBM)
TRIM = pltpu.CompilerParams(vmem_limit_bytes=16 * 2**20)
ROW_BY_ROW = (((1,), (1,)), ((), ()))
BF16 = jnp.bfloat16
F32 = jnp.float32

X, CORE, Z, Y = 4, 2, 32, 4
SHELL = X * CORE
SIDE = 128
PER = 4
PART = SIDE // X
ZR = Z // X
LINES = PER * Z * Y
X0, Y0, Z0 = 2, 2, 17


SLAB = pltpu.VMEM((LINES, SIDE), BF16)


def dmas(count):
    return pltpu.SemaphoreType.DMA((count,))


def iota(shape, axis):
    return lax.broadcasted_iota(jnp.int32, shape, axis)


def one_hot(match):
    return match.astype(BF16)


def dot(a, b):
    return jnp.dot(a, b, preferred_element_type=F32)


def tables_kernel(band_ref, weight_ref, ray_ref, rows_ref, cols_ref, mix_ref, smooth_ref, wide_ref):
    count = SHELL * PER
    band = count // 2
    core = lax.axis_index("core")
    shell, plane = iota((count, count), 0), iota((count, count), 1)
    low = jnp.broadcast_to(band_ref[...], (count, count))
    lanes = jnp.broadcast_to(weight_ref[...], (count, count))
    weight = jnp.sum(jnp.where(shell == plane, lanes, 0.0), axis=1, keepdims=True)
    chi_shell = (shell.astype(F32) + 0.5) / count
    chi_source = (low.astype(F32) + band) / count
    values = 8.0 * weight * chi_shell * (chi_source - chi_shell) / chi_source
    inside = (shell >= low) & (shell < low + band)
    table = jnp.where(inside, values, 0.0).astype(BF16)

    spot, which = iota((LINES, count), 0), iota((LINES, count), 1)
    pick_out = one_hot(which == ((spot // SIDE + X0) % X * CORE + core) * PER + spot % PER)
    spot, which = iota((CORE * LINES, count), 0), iota((CORE * LINES, count), 1)
    source = (spot // (CORE * SIDE) + X0) % X * CORE + spot // SIDE % CORE
    pick_in = one_hot(which == source * PER + spot % PER)
    full = lax.dot_general(dot(pick_out, table).astype(BF16), pick_in, ROW_BY_ROW, preferred_element_type=F32)
    here, there = iota((LINES, CORE * LINES), 0), iota((LINES, CORE * LINES), 1)
    mix_ref[...] = jnp.where(here % SIDE // PER == there % SIDE // PER, full, 0.0).astype(BF16)

    line, lane = iota((LINES, SIDE), 0), iota((LINES, SIDE), 1)
    spread = lax.dot_general(one_hot(lane == line // PER), rows_ref[...], ROW_BY_ROW, preferred_element_type=F32).astype(BF16)
    block = (line % SIDE // PER + Z0) % Z * Y + (line // SIDE + Y0) % Y
    product = lax.dot_general(spread, one_hot(ray_ref[...] == block), ROW_BY_ROW, preferred_element_type=F32)
    here, there = iota((LINES, LINES), 0), iota((LINES, LINES), 1)
    smooth_ref[...] = jnp.where(here % PER == there % PER, product, 0.0).astype(BF16)

    cols = dot(one_hot(lane == (line // SIDE + X0) % X * PART + line % PART), cols_ref[...])
    for y in range(Y):
        wide_ref[:, y * SIDE : (y + 1) * SIDE] = jnp.where(line % SIDE // PART == y, cols, 0.0).astype(BF16)


def swap(slabs):
    return [jnp.concatenate([s[:, k * PART : (k + 1) * PART] for s in slabs], axis=1) for k in range(X)]


def send_kernel(rays_ref, out_ref, rays, slabs, arrived, left):
    cut = Z0 * Y * PER
    pieces = ((cut, 0, LINES - cut), (0, LINES - cut, cut))
    reads = [
        pltpu.make_async_copy(rays_ref.at[pl.ds(start, size)], rays.at[pl.ds(to, size)], arrived.at[k])
        for k, (start, to, size) in enumerate(pieces)
    ]
    for read in reads:
        read.start()
    to, at = iota((SIDE, SIDE), 0), iota((SIDE, SIDE), 1)
    run = ZR * PER
    order = one_hot(at == to % run // PER * (Y * PER) + (to // run + Y0) % Y * PER + to % PER)
    for read in reads:
        read.wait()
    wide = jnp.concatenate([rays[k * SIDE : (k + 1) * SIDE] for k in range(X)], axis=1)
    turned = dot(order, wide)
    parts = swap([turned[:, k * SIDE : (k + 1) * SIDE] for k in range(X)])
    writes = []
    for x in range(X):
        slabs[x * SIDE : (x + 1) * SIDE] = parts[(x + X0) % X].astype(BF16)
        for core in range(CORE):
            k = x * CORE + core
            source = slabs.at[pl.ds(x * SIDE, SIDE)]
            writes.append(pltpu.make_async_copy(source, out_ref.at[pl.ds(k * SIDE, SIDE)], left.at[k]))
            writes[-1].start()
    for write in writes:
        write.wait()


def mix_kernel(mix_ref, planes_ref, out_ref):
    mixed = dot(mix_ref[...], planes_ref[...])
    run = ZR * PER
    for x in range(X):
        rows = [mixed[x * SIDE + y * run : x * SIDE + (y + 1) * run] for y in range(Y)]
        for k, slab in enumerate(swap(rows)):
            at_row = x * SIDE + k * run
            out_ref[at_row : at_row + run] = slab.astype(BF16)


def smooth_kernel(smooth_ref, wide_ref, pixels_ref, out_ref, whole, left):
    pixels = pixels_ref[...]
    flat = jnp.concatenate([pixels[x * SIDE : (x + 1) * SIDE] for x in range(X)], axis=1)
    half = dot(flat, wide_ref[...]).astype(BF16)
    half = jnp.concatenate([half[:, y * SIDE : (y + 1) * SIDE] for y in range(Y)], axis=0)
    part = LINES // 2
    writes = []
    for k in range(2):
        whole[k * part : (k + 1) * part] = dot(smooth_ref[k * part : (k + 1) * part], half).astype(BF16)
        place = pl.ds(k * part, part)
        writes.append(pltpu.make_async_copy(whole.at[place], out_ref.at[place], left.at[k]))
        writes[-1].start()
    for write in writes:
        write.wait()


def call(kernel, name, shapes, *args, ins=VMEM, outs=VMEM, scratch=()):
    out_shape = [jax.ShapeDtypeStruct(shape, BF16) for shape in shapes]
    specs = {"in_specs": [ins] * len(args), "out_specs": [outs] * len(shapes), "scratch_shapes": scratch}
    return pl.pallas_call(kernel, out_shape=out_shape, compiler_params=TRIM, name=name, **specs)(*args)


def shards(residual, tile_ray, filter_rows, filter_cols, band_lo, shell_weight):
    tiles = Z * Y
    mix, smooth, wide = call(
        tables_kernel, "tables", [(LINES, CORE * LINES), (LINES, LINES), (LINES, LINES)],
        band_lo.reshape(1, -1), shell_weight.reshape(1, -1), tile_ray.reshape(1, -1), filter_rows, filter_cols,
    )
    rays = residual.reshape(PER, tiles, SIDE).transpose(1, 0, 2).reshape(LINES, SIDE)
    (send,) = call(
        send_kernel, "send", [(CORE * LINES, SIDE)], rays,
        ins=HBM, outs=HBM, scratch=[SLAB, SLAB, dmas(2), dmas(SHELL)],
    )
    peers = SHELL * Y
    near = [[((X0 + x) % X * CORE + c) * Y + (Y0 + y) % Y for x in range(X) for c in range(CORE) for y in range(Y)]]
    planes = lax.all_to_all(
        send.reshape(peers, -1, SIDE), ("x", "core", "y"), 0, 0, axis_index_groups=near, tiled=True
    )
    (mixed,) = call(mix_kernel, "mix", [(LINES, SIDE)], mix, planes.reshape(CORE * LINES, SIDE))
    far = [[(X0 + x) % X * Z + (Z0 + z) % Z for x in range(X) for z in range(Z)]]
    pixels = lax.all_to_all(
        mixed.reshape(X * Z, PER, SIDE), ("x", "z"), 0, 0, axis_index_groups=far, tiled=True
    )
    (whole,) = call(smooth_kernel, "smooth", [(LINES, SIDE)], smooth, wide, pixels.reshape(LINES, SIDE), outs=HBM, scratch=[SLAB, dmas(2)])
    return whole.reshape(tiles, PER, SIDE).transpose(1, 0, 2).reshape(PER, tiles * SIDE)


def solution(mesh):
    mesh = Mesh(mesh.devices.reshape(X, CORE, Z, Y), ("x", "core", "z", "y"))
    slab = P(("x", "core"), ("z", "y"))
    in_specs = (slab, P(("z", "y")), P(), P(), P(), P())
    return jax.shard_map(shards, mesh=mesh, in_specs=in_specs, out_specs=slab, check_vma=False)
```

```python
import jax
import jax.numpy as jnp
from jax import lax
from jax.experimental import pallas as pl
from jax.experimental.pallas import tpu as pltpu
from jax.sharding import Mesh, PartitionSpec as P

VMEM = pl.BlockSpec(memory_space=pltpu.VMEM)
WHOLE = pltpu.CompilerParams(vmem_limit_bytes=60 * 2**20)
HBM = pl.BlockSpec(memory_space=pltpu.HBM)
TRIM = pltpu.CompilerParams(vmem_limit_bytes=16 * 2**20)
ROW_BY_ROW = (((1,), (1,)), ((), ()))
BF16 = jnp.bfloat16
F32 = jnp.float32

X, CORE, Z, Y = 4, 2, 32, 4
SHELL = X * CORE
SIDE = 128
PER = 4
PART = SIDE // X
ZR = Z // X
LINES = PER * Z * Y
X0, Y0, Z0 = 2, 2, 17


SLAB = pltpu.VMEM((LINES, SIDE), BF16)


def dmas(count):
    return pltpu.SemaphoreType.DMA((count,))


def iota(shape, axis):
    return lax.broadcasted_iota(jnp.int32, shape, axis)


def one_hot(match):
    return match.astype(BF16)


def dot(a, b):
    return jnp.dot(a, b, preferred_element_type=F32)


def tables_kernel(band_ref, weight_ref, ray_ref, rows_ref, cols_ref, mix_ref, smooth_ref, wide_ref):
    count = SHELL * PER
    band = count // 2
    core = lax.axis_index("core")
    shell, plane = iota((count, count), 0), iota((count, count), 1)
    low = jnp.broadcast_to(band_ref[...], (count, count))
    lanes = jnp.broadcast_to(weight_ref[...], (count, count))
    weight = jnp.sum(jnp.where(shell == plane, lanes, 0.0), axis=1, keepdims=True)
    chi_shell = (shell.astype(F32) + 0.5) / count
    chi_source = (low.astype(F32) + band) / count
    values = 8.0 * weight * chi_shell * (chi_source - chi_shell) / chi_source
    inside = (shell >= low) & (shell < low + band)
    table = jnp.where(inside, values, 0.0).astype(BF16)

    part = ZR * PER
    spot, which = iota((X * part, count), 0), iota((X * part, count), 1)
    pick_out = one_hot(which == ((spot // part + X0) % X * CORE + core) * PER + spot % PER)
    spot, which = iota((SHELL * part, count), 0), iota((SHELL * part, count), 1)
    source = (spot // (CORE * part) + X0) % X * CORE + spot // part % CORE
    pick_in = one_hot(which == source * PER + spot % PER)
    full = lax.dot_general(dot(pick_out, table).astype(BF16), pick_in, ROW_BY_ROW, preferred_element_type=F32)
    here, there = iota(full.shape, 0), iota(full.shape, 1)
    mix_ref[...] = jnp.where(here % part // PER == there % part // PER, full, 0.0).astype(BF16)

    line, lane = iota((LINES, SIDE), 0), iota((LINES, SIDE), 1)
    spread = lax.dot_general(one_hot(lane == line // PER), rows_ref[...], ROW_BY_ROW, preferred_element_type=F32).astype(BF16)
    block = (line % SIDE // PER + Z0) % Z * Y + (line // SIDE + Y0) % Y
    product = lax.dot_general(spread, one_hot(ray_ref[...] == block), ROW_BY_ROW, preferred_element_type=F32)
    here, there = iota((LINES, LINES), 0), iota((LINES, LINES), 1)
    smooth_ref[...] = jnp.where(here % PER == there % PER, product, 0.0).astype(BF16)

    cols = dot(one_hot(lane == (line // SIDE + X0) % X * PART + line % PART), cols_ref[...])
    for y in range(Y):
        wide_ref[:, y * SIDE : (y + 1) * SIDE] = jnp.where(line % SIDE // PART == y, cols, 0.0).astype(BF16)


def swap(slabs):
    return [jnp.concatenate([s[:, k * PART : (k + 1) * PART] for s in slabs], axis=1) for k in range(X)]


def send_kernel(rays_ref, out_ref, rays, slabs, arrived, left):
    cut = Z0 * Y * PER
    pieces = ((cut, 0, LINES - cut), (0, LINES - cut, cut))
    reads = [
        pltpu.make_async_copy(rays_ref.at[pl.ds(start, size)], rays.at[pl.ds(to, size)], arrived.at[k])
        for k, (start, to, size) in enumerate(pieces)
    ]
    for read in reads:
        read.start()
    to, at = iota((SIDE, SIDE), 0), iota((SIDE, SIDE), 1)
    run = ZR * PER
    order = one_hot(at == to % run // PER * (Y * PER) + (to // run + Y0) % Y * PER + to % PER)
    for read in reads:
        read.wait()
    wide = jnp.concatenate([rays[k * SIDE : (k + 1) * SIDE] for k in range(X)], axis=1)
    turned = dot(order, wide)
    parts = swap([turned[:, k * SIDE : (k + 1) * SIDE] for k in range(X)])
    writes = []
    for x in range(X):
        slabs[x * SIDE : (x + 1) * SIDE] = parts[(x + X0) % X].astype(BF16)
        for core in range(CORE):
            k = x * CORE + core
            source = slabs.at[pl.ds(x * SIDE, SIDE)]
            writes.append(pltpu.make_async_copy(source, out_ref.at[pl.ds(k * SIDE, SIDE)], left.at[k]))
            writes[-1].start()
    for write in writes:
        write.wait()


def mix_kernel(mix_ref, planes_ref, out_ref):
    part = ZR * PER
    by_y = []
    for y in range(Y):
        spots = [g * SIDE + y * part for g in range(SHELL)]
        by_y.append(jnp.concatenate([planes_ref[spot : spot + part] for spot in spots], axis=0))
    mixed = dot(mix_ref[...], jnp.concatenate(by_y, axis=1))
    for k, slab in enumerate(swap([mixed[:, y * SIDE : (y + 1) * SIDE] for y in range(Y)])):
        slab = slab.astype(BF16)
        for x in range(X):
            spot = x * SIDE + k * part
            out_ref[spot : spot + part] = slab[x * part : (x + 1) * part]


def smooth_kernel(smooth_ref, wide_ref, pixels_ref, out_ref, whole, left):
    pixels = pixels_ref[...]
    flat = jnp.concatenate([pixels[x * SIDE : (x + 1) * SIDE] for x in range(X)], axis=1)
    half = dot(flat, wide_ref[...]).astype(BF16)
    half = jnp.concatenate([half[:, y * SIDE : (y + 1) * SIDE] for y in range(Y)], axis=0)
    part = LINES // 2
    writes = []
    for k in range(2):
        whole[k * part : (k + 1) * part] = dot(smooth_ref[k * part : (k + 1) * part], half).astype(BF16)
        place = pl.ds(k * part, part)
        writes.append(pltpu.make_async_copy(whole.at[place], out_ref.at[place], left.at[k]))
        writes[-1].start()
    for write in writes:
        write.wait()


def call(kernel, name, shapes, *args, ins=VMEM, outs=VMEM, scratch=(), params=TRIM):
    out_shape = [jax.ShapeDtypeStruct(shape, BF16) for shape in shapes]
    specs = {"in_specs": [ins] * len(args), "out_specs": [outs] * len(shapes), "scratch_shapes": scratch}
    return pl.pallas_call(kernel, out_shape=out_shape, compiler_params=params, name=name, **specs)(*args)


def shards(residual, tile_ray, filter_rows, filter_cols, band_lo, shell_weight):
    tiles = Z * Y
    mix, smooth, wide = call(
        tables_kernel, "tables", [(SIDE, 2 * SIDE), (LINES, LINES), (LINES, LINES)],
        band_lo.reshape(1, -1), shell_weight.reshape(1, -1), tile_ray.reshape(1, -1), filter_rows, filter_cols,
    )
    rays = residual.reshape(PER, tiles, SIDE).transpose(1, 0, 2).reshape(LINES, SIDE)
    (send,) = call(
        send_kernel, "send", [(CORE * LINES, SIDE)], rays,
        ins=HBM, outs=HBM, scratch=[SLAB, SLAB, dmas(2), dmas(SHELL)], params=WHOLE,
    )
    peers = SHELL * Y
    near = [[((X0 + x) % X * CORE + c) * Y + (Y0 + y) % Y for x in range(X) for c in range(CORE) for y in range(Y)]]
    planes = lax.all_to_all(
        send.reshape(peers, -1, SIDE), ("x", "core", "y"), 0, 0, axis_index_groups=near, tiled=True
    )
    (mixed,) = call(mix_kernel, "mix", [(LINES, SIDE)], mix, planes.reshape(CORE * LINES, SIDE))
    far = [[(X0 + x) % X * Z + (Z0 + z) % Z for x in range(X) for z in range(Z)]]
    pixels = lax.all_to_all(
        mixed.reshape(X * Z, PER, SIDE), ("x", "z"), 0, 0, axis_index_groups=far, tiled=True
    )
    (whole,) = call(smooth_kernel, "smooth", [(LINES, SIDE)], smooth, wide, pixels.reshape(LINES, SIDE), outs=HBM, scratch=[SLAB, dmas(2)])
    return whole.reshape(tiles, PER, SIDE).transpose(1, 0, 2).reshape(PER, tiles * SIDE)


def solution(mesh):
    mesh = Mesh(mesh.devices.reshape(X, CORE, Z, Y), ("x", "core", "z", "y"))
    slab = P(("x", "core"), ("z", "y"))
    in_specs = (slab, P(("z", "y")), P(), P(), P(), P())
    return jax.shard_map(shards, mesh=mesh, in_specs=in_specs, out_specs=slab, check_vma=False)
```

```python
import jax
import jax.numpy as jnp
from jax import lax
from jax.experimental import pallas as pl
from jax.experimental.pallas import tpu as pltpu
from jax.sharding import Mesh, PartitionSpec as P

VMEM = pl.BlockSpec(memory_space=pltpu.VMEM)
WHOLE = pltpu.CompilerParams(vmem_limit_bytes=60 * 2**20)
HBM = pl.BlockSpec(memory_space=pltpu.HBM)
TRIM = pltpu.CompilerParams(vmem_limit_bytes=16 * 2**20)
ROW_BY_ROW = (((1,), (1,)), ((), ()))
BF16 = jnp.bfloat16
F32 = jnp.float32

X, CORE, Z, Y = 4, 2, 32, 4
SHELL = X * CORE
SIDE = 128
PER = 4
PART = SIDE // X
ZR = Z // X
LINES = PER * Z * Y
X0, Y0, Z0 = 2, 2, 17


SLAB = pltpu.VMEM((LINES, SIDE), BF16)


def dmas(count):
    return pltpu.SemaphoreType.DMA((count,))


def iota(shape, axis):
    return lax.broadcasted_iota(jnp.int32, shape, axis)


def one_hot(match):
    return match.astype(BF16)


def dot(a, b):
    return jnp.dot(a, b, preferred_element_type=F32)


def fill_tables(band_ref, weight_ref, ray_ref, rows_ref, cols_ref, mix_ref, smooth_ref, wide_ref):
    count = SHELL * PER
    band = count // 2
    core = lax.axis_index("core")
    shell, plane = iota((count, count), 0), iota((count, count), 1)
    low = jnp.broadcast_to(band_ref[...], (count, count))
    lanes = jnp.broadcast_to(weight_ref[...], (count, count))
    weight = jnp.sum(jnp.where(shell == plane, lanes, 0.0), axis=1, keepdims=True)
    chi_shell = (shell.astype(F32) + 0.5) / count
    chi_source = (low.astype(F32) + band) / count
    values = 8.0 * weight * chi_shell * (chi_source - chi_shell) / chi_source
    inside = (shell >= low) & (shell < low + band)
    table = jnp.where(inside, values, 0.0).astype(BF16)

    part = ZR * PER
    spot, which = iota((X * part, count), 0), iota((X * part, count), 1)
    pick_out = one_hot(which == ((spot // part + X0) % X * CORE + core) * PER + spot % PER)
    spot, which = iota((SHELL * part, count), 0), iota((SHELL * part, count), 1)
    source = (spot // (CORE * part) + X0) % X * CORE + spot // part % CORE
    pick_in = one_hot(which == source * PER + spot % PER)
    full = lax.dot_general(dot(pick_out, table).astype(BF16), pick_in, ROW_BY_ROW, preferred_element_type=F32)
    here, there = iota(full.shape, 0), iota(full.shape, 1)
    mix_ref[...] = jnp.where(here % part // PER == there % part // PER, full, 0.0).astype(BF16)

    line, lane = iota((LINES, SIDE), 0), iota((LINES, SIDE), 1)
    spread = lax.dot_general(one_hot(lane == line // PER), rows_ref[...], ROW_BY_ROW, preferred_element_type=F32).astype(BF16)
    block = (line % SIDE // PER + Z0) % Z * Y + (line // SIDE + Y0) % Y
    product = lax.dot_general(spread, one_hot(ray_ref[...] == block), ROW_BY_ROW, preferred_element_type=F32)
    here, there = iota((LINES, LINES), 0), iota((LINES, LINES), 1)
    smooth_ref[...] = jnp.where(here % PER == there % PER, product, 0.0).astype(BF16)

    cols = dot(one_hot(lane == (line // SIDE + X0) % X * PART + line % PART), cols_ref[...])
    for y in range(Y):
        wide_ref[:, y * SIDE : (y + 1) * SIDE] = jnp.where(line % SIDE // PART == y, cols, 0.0).astype(BF16)


def swap(slabs):
    return [jnp.concatenate([s[:, k * PART : (k + 1) * PART] for s in slabs], axis=1) for k in range(X)]


def open_kernel(*refs):
    given, rays_ref = refs[:5], refs[5]
    tables, out_ref = refs[6:9], refs[9]
    held, rays, arrived = refs[10:15], refs[15], refs[16]
    cut = Z0 * Y * PER
    small = [pltpu.make_async_copy(src, dst, arrived.at[k]) for k, (src, dst) in enumerate(zip(given, held))]
    reads = [
        pltpu.make_async_copy(rays_ref.at[pl.ds(start, size)], rays.at[pl.ds(to, size)], arrived.at[5 + k])
        for k, (start, to, size) in enumerate(((cut, 0, LINES - cut), (0, LINES - cut, cut)))
    ]
    for read in small + reads:
        read.start()
    to, at = iota((SIDE, SIDE), 0), iota((SIDE, SIDE), 1)
    run = ZR * PER
    order = one_hot(at == to % run // PER * (Y * PER) + (to // run + Y0) % Y * PER + to % PER)
    for read in small:
        read.wait()
    fill_tables(*held, *tables)
    for read in reads:
        read.wait()
    wide = jnp.concatenate([rays[k * SIDE : (k + 1) * SIDE] for k in range(X)], axis=1)
    turned = dot(order, wide)
    parts = swap([turned[:, k * SIDE : (k + 1) * SIDE] for k in range(X)])
    for x in range(X):
        slab = parts[(x + X0) % X].astype(BF16)
        for core in range(CORE):
            at_row = (x * CORE + core) * SIDE
            out_ref[at_row : at_row + SIDE] = slab


def mix_kernel(mix_ref, planes_ref, out_ref):
    part = ZR * PER
    by_y = []
    for y in range(Y):
        spots = [g * SIDE + y * part for g in range(SHELL)]
        by_y.append(jnp.concatenate([planes_ref[spot : spot + part] for spot in spots], axis=0))
    mixed = dot(mix_ref[...], jnp.concatenate(by_y, axis=1))
    for k, slab in enumerate(swap([mixed[:, y * SIDE : (y + 1) * SIDE] for y in range(Y)])):
        slab = slab.astype(BF16)
        for x in range(X):
            spot = x * SIDE + k * part
            out_ref[spot : spot + part] = slab[x * part : (x + 1) * part]


def smooth_kernel(smooth_ref, wide_ref, pixels_ref, out_ref, whole, left):
    pixels = pixels_ref[...]
    flat = jnp.concatenate([pixels[x * SIDE : (x + 1) * SIDE] for x in range(X)], axis=1)
    half = dot(flat, wide_ref[...]).astype(BF16)
    half = jnp.concatenate([half[:, y * SIDE : (y + 1) * SIDE] for y in range(Y)], axis=0)
    part = LINES // 2
    writes = []
    for k in range(2):
        whole[k * part : (k + 1) * part] = dot(smooth_ref[k * part : (k + 1) * part], half).astype(BF16)
        place = pl.ds(k * part, part)
        writes.append(pltpu.make_async_copy(whole.at[place], out_ref.at[place], left.at[k]))
        writes[-1].start()
    for write in writes:
        write.wait()


def call(kernel, name, shapes, *args, ins=VMEM, outs=VMEM, scratch=(), params=TRIM):
    out_shape = [jax.ShapeDtypeStruct(shape, BF16) for shape in shapes]
    specs = {"in_specs": [ins] * len(args), "out_specs": [outs] * len(shapes), "scratch_shapes": scratch}
    return pl.pallas_call(kernel, out_shape=out_shape, compiler_params=params, name=name, **specs)(*args)


def shards(residual, tile_ray, filter_rows, filter_cols, band_lo, shell_weight):
    tiles = Z * Y
    rays = residual.reshape(PER, tiles, SIDE).transpose(1, 0, 2).reshape(LINES, SIDE)
    given = (band_lo.reshape(1, -1), shell_weight.reshape(1, -1), tile_ray.reshape(1, -1), filter_rows, filter_cols)
    held = [pltpu.VMEM(arg.shape, arg.dtype) for arg in given]
    mix, smooth, wide, send = call(
        open_kernel, "open", [(SIDE, 2 * SIDE), (LINES, LINES), (LINES, LINES), (CORE * LINES, SIDE)], *[pltpu.with_memory_space_constraint(arg, pltpu.HBM) for arg in (*given, rays)],
        ins=HBM, scratch=[*held, SLAB, dmas(7)],
    )
    peers = SHELL * Y
    near = [[((X0 + x) % X * CORE + c) * Y + (Y0 + y) % Y for x in range(X) for c in range(CORE) for y in range(Y)]]
    planes = lax.all_to_all(
        send.reshape(peers, -1, SIDE), ("x", "core", "y"), 0, 0, axis_index_groups=near, tiled=True
    )
    (mixed,) = call(mix_kernel, "mix", [(LINES, SIDE)], mix, planes.reshape(CORE * LINES, SIDE))
    far = [[(X0 + x) % X * Z + (Z0 + z) % Z for x in range(X) for z in range(Z)]]
    pixels = lax.all_to_all(
        mixed.reshape(X * Z, PER, SIDE), ("x", "z"), 0, 0, axis_index_groups=far, tiled=True
    )
    (whole,) = call(smooth_kernel, "smooth", [(LINES, SIDE)], smooth, wide, pixels.reshape(LINES, SIDE), outs=HBM, scratch=[SLAB, dmas(2)])
    return whole.reshape(tiles, PER, SIDE).transpose(1, 0, 2).reshape(PER, tiles * SIDE)


def solution(mesh):
    mesh = Mesh(mesh.devices.reshape(X, CORE, Z, Y), ("x", "core", "z", "y"))
    slab = P(("x", "core"), ("z", "y"))
    in_specs = (slab, P(("z", "y")), P(), P(), P(), P())
    return jax.shard_map(shards, mesh=mesh, in_specs=in_specs, out_specs=slab, check_vma=False)
```

```python
import jax
import jax.numpy as jnp
from jax import lax
from jax.experimental import pallas as pl
from jax.experimental.pallas import tpu as pltpu
from jax.sharding import Mesh, PartitionSpec as P

VMEM = pl.BlockSpec(memory_space=pltpu.VMEM)
WHOLE = pltpu.CompilerParams(vmem_limit_bytes=60 * 2**20)
HBM = pl.BlockSpec(memory_space=pltpu.HBM)
TRIM = pltpu.CompilerParams(vmem_limit_bytes=16 * 2**20)
ROW_BY_ROW = (((1,), (1,)), ((), ()))
BF16 = jnp.bfloat16
F32 = jnp.float32

X, CORE, Z, Y = 4, 2, 32, 4
SHELL = X * CORE
SIDE = 128
PER = 4
PART = SIDE // X
ZR = Z // X
LINES = PER * Z * Y
X0, Y0, Z0 = 2, 2, 18


SLAB = pltpu.VMEM((LINES, SIDE), BF16)


def dmas(count):
    return pltpu.SemaphoreType.DMA((count,))


def iota(shape, axis):
    return lax.broadcasted_iota(jnp.int32, shape, axis)


def one_hot(match):
    return match.astype(BF16)


def dot(a, b):
    return jnp.dot(a, b, preferred_element_type=F32)


def patterns():
    count, part = SHELL * PER, ZR * PER
    core = lax.axis_index("core")
    spot, which = iota((X * part, count), 0), iota((X * part, count), 1)
    pick_out = one_hot(which == ((spot // part + X0) % X * CORE + core) * PER + spot % PER)
    spot, which = iota((SHELL * part, count), 0), iota((SHELL * part, count), 1)
    source = (spot // (CORE * part) + X0) % X * CORE + spot // part % CORE
    pick_in = one_hot(which == source * PER + spot % PER)
    line, lane = iota((LINES, SIDE), 0), iota((LINES, SIDE), 1)
    pixel = one_hot(lane == line // PER)
    column = one_hot(lane == (line // SIDE + X0) % X * PART + line % PART)
    return pick_out, pick_in, pixel, column


def fill_tables(ready, band_ref, weight_ref, ray_ref, rows_ref, cols_ref, mix_ref, smooth_ref, wide_ref):
    pick_out, pick_in, pixel, column = ready
    count, part = SHELL * PER, ZR * PER
    band = count // 2
    shell, plane = iota((count, count), 0), iota((count, count), 1)
    low = jnp.broadcast_to(band_ref[...], (count, count))
    lanes = jnp.broadcast_to(weight_ref[...], (count, count))
    weight = jnp.sum(jnp.where(shell == plane, lanes, 0.0), axis=1, keepdims=True)
    chi_shell = (shell.astype(F32) + 0.5) / count
    chi_source = (low.astype(F32) + band) / count
    values = 8.0 * weight * chi_shell * (chi_source - chi_shell) / chi_source
    inside = (shell >= low) & (shell < low + band)
    table = jnp.where(inside, values, 0.0).astype(BF16)
    full = lax.dot_general(dot(pick_out, table).astype(BF16), pick_in, ROW_BY_ROW, preferred_element_type=F32)
    here, there = iota(full.shape, 0), iota(full.shape, 1)
    mix_ref[...] = jnp.where(here % part // PER == there % part // PER, full, 0.0).astype(BF16)

    line = iota((LINES, SIDE), 0)
    spread = lax.dot_general(pixel, rows_ref[...], ROW_BY_ROW, preferred_element_type=F32).astype(BF16)
    block = (line % SIDE // PER + Z0) % Z * Y + (line // SIDE + Y0) % Y
    product = lax.dot_general(spread, one_hot(ray_ref[...] == block), ROW_BY_ROW, preferred_element_type=F32)
    here, there = iota((LINES, LINES), 0), iota((LINES, LINES), 1)
    smooth_ref[...] = jnp.where(here % PER == there % PER, product, 0.0).astype(BF16)

    cols = dot(column, cols_ref[...])
    for y in range(Y):
        wide_ref[:, y * SIDE : (y + 1) * SIDE] = jnp.where(line % SIDE // PART == y, cols, 0.0).astype(BF16)


def swap(slabs):
    return [jnp.concatenate([s[:, k * PART : (k + 1) * PART] for s in slabs], axis=1) for k in range(X)]


def open_kernel(*refs):
    given, rays_ref = refs[:5], refs[5]
    tables, out_ref = refs[6:9], refs[9]
    held, rays, arrived = refs[10:15], refs[15], refs[16]
    cut = Z0 * Y * PER
    small = [pltpu.make_async_copy(src, dst, arrived.at[k]) for k, (src, dst) in enumerate(zip(given, held))]
    reads = [
        pltpu.make_async_copy(rays_ref.at[pl.ds(start, size)], rays.at[pl.ds(to, size)], arrived.at[5 + k])
        for k, (start, to, size) in enumerate(((cut, 0, LINES - cut), (0, LINES - cut, cut)))
    ]
    for read in small + reads:
        read.start()
    to, at = iota((SIDE, SIDE), 0), iota((SIDE, SIDE), 1)
    run = ZR * PER
    order = one_hot(at == to % run // PER * (Y * PER) + (to // run + Y0) % Y * PER + to % PER)
    ready = patterns()
    for read in small:
        read.wait()
    fill_tables(ready, *held, *tables)
    for read in reads:
        read.wait()
    wide = jnp.concatenate([rays[k * SIDE : (k + 1) * SIDE] for k in range(X)], axis=1)
    turned = dot(order, wide)
    parts = swap([turned[:, k * SIDE : (k + 1) * SIDE] for k in range(X)])
    for x in range(X):
        slab = parts[(x + X0) % X].astype(BF16)
        for core in range(CORE):
            at_row = (x * CORE + core) * SIDE
            out_ref[at_row : at_row + SIDE] = slab


def mix_kernel(mix_ref, planes_ref, out_ref):
    part = ZR * PER
    by_y = []
    for y in range(Y):
        spots = [g * SIDE + y * part for g in range(SHELL)]
        by_y.append(jnp.concatenate([planes_ref[spot : spot + part] for spot in spots], axis=0))
    mixed = dot(mix_ref[...], jnp.concatenate(by_y, axis=1))
    for k, slab in enumerate(swap([mixed[:, y * SIDE : (y + 1) * SIDE] for y in range(Y)])):
        slab = slab.astype(BF16)
        for x in range(X):
            spot = x * SIDE + k * part
            out_ref[spot : spot + part] = slab[x * part : (x + 1) * part]


def smooth_kernel(smooth_ref, wide_ref, pixels_ref, out_ref, whole, left):
    pixels = pixels_ref[...]
    flat = jnp.concatenate([pixels[x * SIDE : (x + 1) * SIDE] for x in range(X)], axis=1)
    half = dot(flat, wide_ref[...]).astype(BF16)
    half = jnp.concatenate([half[:, y * SIDE : (y + 1) * SIDE] for y in range(Y)], axis=0)
    part = LINES // 2
    writes = []
    for k in range(2):
        whole[k * part : (k + 1) * part] = dot(smooth_ref[k * part : (k + 1) * part], half).astype(BF16)
        place = pl.ds(k * part, part)
        writes.append(pltpu.make_async_copy(whole.at[place], out_ref.at[place], left.at[k]))
        writes[-1].start()
    for write in writes:
        write.wait()


def call(kernel, name, shapes, *args, ins=VMEM, outs=VMEM, scratch=(), params=TRIM):
    out_shape = [jax.ShapeDtypeStruct(shape, BF16) for shape in shapes]
    specs = {"in_specs": [ins] * len(args), "out_specs": [outs] * len(shapes), "scratch_shapes": scratch}
    return pl.pallas_call(kernel, out_shape=out_shape, compiler_params=params, name=name, **specs)(*args)


def shards(residual, tile_ray, filter_rows, filter_cols, band_lo, shell_weight):
    tiles = Z * Y
    rays = residual.reshape(PER, tiles, SIDE).transpose(1, 0, 2).reshape(LINES, SIDE)
    given = (band_lo.reshape(1, -1), shell_weight.reshape(1, -1), tile_ray.reshape(1, -1), filter_rows, filter_cols)
    held = [pltpu.VMEM(arg.shape, arg.dtype) for arg in given]
    mix, smooth, wide, send = call(
        open_kernel, "open", [(SIDE, 2 * SIDE), (LINES, LINES), (LINES, LINES), (CORE * LINES, SIDE)], *[pltpu.with_memory_space_constraint(arg, pltpu.HBM) for arg in (*given, rays)],
        ins=HBM, scratch=[*held, SLAB, dmas(7)],
    )
    peers = SHELL * Y
    near = [[((X0 + x) % X * CORE + c) * Y + (Y0 + y) % Y for x in range(X) for c in range(CORE) for y in range(Y)]]
    planes = lax.all_to_all(
        send.reshape(peers, -1, SIDE), ("x", "core", "y"), 0, 0, axis_index_groups=near, tiled=True
    )
    (mixed,) = call(mix_kernel, "mix", [(LINES, SIDE)], mix, planes.reshape(CORE * LINES, SIDE))
    far = [[(X0 + x) % X * Z + (Z0 + z) % Z for x in range(X) for z in range(Z)]]
    pixels = lax.all_to_all(
        mixed.reshape(X * Z, PER, SIDE), ("x", "z"), 0, 0, axis_index_groups=far, tiled=True
    )
    (whole,) = call(smooth_kernel, "smooth", [(LINES, SIDE)], smooth, wide, pixels.reshape(LINES, SIDE), outs=HBM, scratch=[SLAB, dmas(2)])
    return whole.reshape(tiles, PER, SIDE).transpose(1, 0, 2).reshape(PER, tiles * SIDE)


def solution(mesh):
    mesh = Mesh(mesh.devices.reshape(X, CORE, Z, Y), ("x", "core", "z", "y"))
    slab = P(("x", "core"), ("z", "y"))
    in_specs = (slab, P(("z", "y")), P(), P(), P(), P())
    return jax.shard_map(shards, mesh=mesh, in_specs=in_specs, out_specs=slab, check_vma=False)
```
